32 devices in a mesh: dp: 8 (over z, y), rep: 4 (over x, core).
Axes of the slice: x: 2, y: 2, z: 4, core: 2. Of those that a mesh axis runs over, the one named last changes fastest.
Arguments:
- cell_input: bfloat16 [16384, 1024], P(('dp', 'rep')), may hold values from -6 to 6
- cotangent: bfloat16 [16384, 1024], P(('dp', 'rep')), may hold values from -6 to 6
- segment_ids: int32 [32, 512], P(('dp', 'rep')), may hold values from 0 to 15, never falling along the last dimension, each value on 1 to 128 neighbouring positions
- lengths: int32 [32], P(('dp', 'rep')), may hold values from 256 to 512
- w_qkv: bfloat16 [1024, 3072], P('dp'), may hold values from -0.1875 to 0.1875
- query_bias: bfloat16 [1024], P('dp'), may hold values from -1.75 to 1.75
- value_bias: bfloat16 [1024], P('dp'), may hold values from -1.75 to 1.75
- w_out: bfloat16 [1024, 1024], P('dp'), may hold values from -1 to 1
- out_bias: bfloat16 [1024], P('dp'), may hold values from -1.75 to 1.75
- w_up: bfloat16 [1024, 4096], P('dp'), may hold values from -0.1875 to 0.1875
- up_bias: bfloat16 [4096], P('dp'), may hold values from -1.75 to 1.75
- w_down: bfloat16 [4096, 1024], P('dp'), may hold values from -0.09375 to 0.09375
- down_bias: bfloat16 [1024], P('dp'), may hold values from -1.75 to 1.75
- norm1_gain: bfloat16 [1024], P('dp'), may hold values from 0.5 to 1.5
- norm1_bias: bfloat16 [1024], P('dp'), may hold values from -1.75 to 1.75
- norm2_gain: bfloat16 [1024], P('dp'), may hold values from 0.5 to 1.5
- norm2_bias: bfloat16 [1024], P('dp'), may hold values from -1.75 to 1.75
Outputs:
- block_out: bfloat16 [16384, 1024], P(('dp', 'rep'))
- input_grad: bfloat16 [16384, 1024], P(('dp', 'rep'))
- grad_qkv: float32 [1024, 3072], P('dp')
- grad_query_bias: float32 [1024], P('dp')
- grad_value_bias: float32 [1024], P('dp')
- grad_out: float32 [1024, 1024], P('dp')
- grad_out_bias: float32 [1024], P('dp')
- grad_up: float32 [1024, 4096], P('dp')
- grad_up_bias: float32 [4096], P('dp')
- grad_down: float32 [4096, 1024], P('dp')
- grad_down_bias: float32 [1024], P('dp')
- grad_norm1_gain: float32 [1024], P('dp')
- grad_norm1_bias: float32 [1024], P('dp')
- grad_norm2_gain: float32 [1024], P('dp')
- grad_norm2_bias: float32 [1024], P('dp')
The draws below stay inside these ranges and needn't reach their ends.
Inputs may be any that keep to these rules, and one draw needn't show every extreme that they name: `segment_ids`: in each sequence the ids never fall; each of the 16 slides holds 1 to 128 cells, and one holds exactly 128. `lengths`: rows of a sequence at or past its length are padding.
All inputs are finite; a program needn't handle non-finite values.
Results may differ from the reference program's by a relative error of at most 0.015.
Values may be sent and summed in bfloat16 or wider, within the bound.
No kernel may reach another device: no remote copies, remote signals or barrier semaphores. Data moves between devices by JAX's collectives and lax.ppermute only.
A program may use at most 192 MiB of HBM per device.

```python
import math
import jax
import jax.numpy as jnp
import numpy as np
from jax import lax

D = 1024
HEAD_DIM = 64
FF = 4096
TOK_DEV = 512
SLIDES = 16
SLIDE_MOST = 128
SEQS = 32
TOKENS = 16384


def touch_ends(values, stream_key, least, high):
    shape = values.shape
    place = [jax.random.randint(jax.random.fold_in(stream_key, axis), (), 0, shape[axis]) for axis in range(len(shape))]
    values = values.at[tuple(place)].set(least)
    longest = shape.index(max(shape))
    place[longest] = (place[longest] + 1) % shape[longest]
    return values.at[tuple(place)].set(high)


def raised(array, rng, source, target, blocks, factor):
    owner, partner = [(jnp.arange(array.shape[position]) // (array.shape[position] // blocks)).reshape([-1 if axis == position else 1 for axis in range(array.ndim)]) for position in (source, target)]
    chosen = jax.random.permutation(rng, blocks)[partner]
    strong = (owner == chosen) | (owner == (partner + blocks // 2) % blocks)
    return jnp.where(strong, factor * array, array)


def steps_of(stream_key, shape, cuts, least, high):
    level = 1.0
    for position, blocks in cuts:
        steps = jax.random.uniform(jax.random.fold_in(jax.random.fold_in(stream_key, 6), position), (blocks,), jnp.float32, least / len(cuts), high / len(cuts))
        level = level * jnp.repeat(jnp.exp(steps), shape[position] // blocks).reshape((-1,) + (1,) * (len(shape) - 1 - position))
    return level


def split_up(count, total, limit, skew):
    portions = [(1 << 20) // math.isqrt(grade ** skew) + 1 for grade in range(2, count + 1)]
    rest, holding = total - limit - (count - 1), [1] * (count - 1)
    while rest > 0:
        candidates = [i for i in range(count - 1) if holding[i] < limit]
        pool, left = sum([portions[i] for i in candidates]), rest
        for i in candidates:
            more = min(limit - holding[i], max(1, left * portions[i] // pool), rest)
            holding[i] = holding[i] + more
            rest = rest - more
    return np.array([limit] + holding)


def uneven(stream_key, amount, total, reach, skew):
    if amount == 2:
        one = jax.random.randint(stream_key, (), max(1, total - reach), min(reach, total - 1) + 1)
        return jnp.stack([one, total - one])
    sizes = jnp.asarray(split_up(amount, total, reach, skew), jnp.int32)
    pairs = (amount - 1) // 2
    giver, taker = sizes[1:1 + 2 * pairs:2], sizes[2:2 + 2 * pairs:2]
    room = jnp.minimum(giver - 1, reach - taker)
    passed = jax.random.randint(jax.random.fold_in(stream_key, 1), (pairs,), 0, 1 << 20) % (room + 1)
    sizes = sizes.at[1:1 + 2 * pairs:2].set(giver - passed).at[2:2 + 2 * pairs:2].set(taker + passed)
    return sizes[jax.random.permutation(jax.random.fold_in(stream_key, 2), amount)]


def gaussian(key, extent, spread, bound, pieces=(), held_as=jnp.bfloat16):
    entries = jax.random.normal(key, extent, jnp.float32) * spread
    if len(pieces) > 0:
        entries = steps_of(key, extent, pieces, -0.22, 0.18) * entries
    return jnp.clip(entries, min=-bound, max=bound).astype(held_as)


def noise_with(rng, dims, width, reach, shards, heavy, held_as=jnp.bfloat16):
    entries = width * jax.random.normal(rng, dims, jnp.float32)
    if shards:
        entries = entries * steps_of(rng, dims, shards, -0.22, 0.18)
    return jnp.clip(raised(entries, jax.random.fold_in(rng, 3), *heavy), -reach, reach).astype(held_as)


def setup_inputs(seed: int = 0) -> dict:
    splits = jax.random.split(jax.random.key(seed), 18)
    return {
        "cell_input": gaussian(splits[0], (TOKENS, D), 1.0, 6.0, ((0, 32),)),
        "cotangent": noise_with(splits[1], (TOKENS, D), 1.0, 6.0, ((0, 32),), (0, 1, 32, 2.75)),
        "segment_ids": jax.vmap(lambda own: jnp.searchsorted(jnp.cumsum(uneven(own, SLIDES, TOK_DEV, SLIDE_MOST, 2)), jnp.arange(TOK_DEV), side="right"))(jax.random.split(splits[2], SEQS)).reshape((SEQS, TOK_DEV)).astype(jnp.int32),
        "lengths": touch_ends(jax.random.randint(splits[3], (SEQS,), TOK_DEV // 2, TOK_DEV + 1), jax.random.fold_in(splits[3], 1), TOK_DEV // 2, TOK_DEV).astype(jnp.int32),
        "w_qkv": gaussian(splits[4], (D, 3 * D), D ** -0.5, 0.1875, ((0, 8),)),
        "query_bias": gaussian(splits[5], (D,), 0.3, 1.75, ((0, 8),)),
        "value_bias": gaussian(splits[6], (D,), 0.3, 1.75, ((0, 8),)),
        "w_out": gaussian(splits[7], (D, D), (D // 32) ** -0.5, 1.0, ((0, 8),)),
        "out_bias": gaussian(splits[8], (D,), 0.3, 1.75, ((0, 8),)),
        "w_up": gaussian(splits[9], (D, FF), D ** -0.5, 0.1875, ((0, 8),)),
        "up_bias": gaussian(splits[10], (FF,), 0.3, 1.75, ((0, 8),)),
        "w_down": gaussian(splits[11], (FF, D), FF ** -0.5, 0.09375, ((0, 8),)),
        "down_bias": gaussian(splits[12], (D,), 0.3, 1.75, ((0, 8),)),
        "norm1_gain": jnp.clip(1.0 + 0.1 * jax.random.normal(splits[13], (D,), jnp.float32), 0.5, 1.5).astype(jnp.bfloat16),
        "norm1_bias": gaussian(splits[14], (D,), 0.3, 1.75, ((0, 8),)),
        "norm2_gain": jnp.clip(1.0 + 0.1 * jax.random.normal(splits[15], (D,), jnp.float32), 0.5, 1.5).astype(jnp.bfloat16),
        "norm2_bias": gaussian(splits[16], (D,), 0.3, 1.75, ((0, 8),)),
    }


@jax.custom_vjp
def low(v):
    return lax.optimization_barrier(v.astype(jnp.bfloat16)).astype(jnp.float32)

@jax.custom_vjp
def low_back(v):
    return v

def low_keep(v):
    return (low(v), None)

def low_pass(kept, grad):
    return (grad,)

def back_keep(v):
    return (v, None)

def back_low(kept, grad):
    return (low(grad),)
low.defvjp(low_keep, low_pass)
low_back.defvjp(back_keep, back_low)
precise = lax.Precision.HIGHEST

def normalize(values_in):
    row_mean = lax.optimization_barrier(jnp.mean(values_in, axis=-1, keepdims=True))
    centred = values_in - row_mean
    return centred * lax.rsqrt(lax.optimization_barrier(jnp.mean(centred * centred, axis=-1, keepdims=True)) + 1e-05)

def positions(length, model_width):
    places = jnp.arange(length, dtype=jnp.float32)[:, None]
    frequency = jnp.exp(jnp.arange(model_width // 2, dtype=jnp.float32) * (-2.0 * math.log(10000.0) / model_width))
    angles = places * frequency[None, :]
    return jnp.stack([jnp.sin(angles), jnp.cos(angles)], axis=-1).reshape(length, model_width)

def block(params, cell_rows, pos_table, allowed):
    w_qkv, query_bias, value_bias, w_out, out_bias, w_up, up_bias, w_down, down_bias, norm1_gain, norm1_bias, norm2_gain, norm2_bias = params
    groups, length, model_width = cell_rows.shape
    head_count = model_width // HEAD_DIM
    score_scale = 1.0 / math.sqrt(HEAD_DIM)
    normed_in = low(normalize(cell_rows) * norm1_gain + norm1_bias + pos_table)
    projected = jnp.einsum('gtd,de->gte', normed_in, w_qkv, precision=precise)
    queries = low_back(low(projected[..., :model_width] + query_bias)).reshape(groups, length, head_count, HEAD_DIM)
    key_vecs = low_back(low(projected[..., model_width:2 * model_width])).reshape(groups, length, head_count, HEAD_DIM)
    values = low_back(low(projected[..., 2 * model_width:] + value_bias)).reshape(groups, length, head_count, HEAD_DIM)
    scores = jnp.einsum('gqhd,gkhd->ghqk', queries, key_vecs, precision=precise) * score_scale
    scores = jnp.where(allowed[:, None], low_back(scores), -1e+30)
    weights = jax.nn.softmax(scores, axis=-1)
    attended = jnp.einsum('ghqk,gkhd->gqhd', low(weights), values, precision=precise).reshape(groups, length, model_width)
    attended = low_back(low(attended))
    branch = low_back(jnp.einsum('gtd,de->gte', attended, w_out, precision=precise) + out_bias)
    middle = cell_rows + branch
    hidden_in = low(normalize(middle) * norm2_gain + norm2_bias)
    pre_act = low_back(jnp.einsum('gtd,df->gtf', hidden_in, w_up, precision=precise) + up_bias)
    hidden = low(jax.nn.gelu(pre_act, approximate=False))
    branch_two = low_back(jnp.einsum('gtf,fd->gtd', hidden, w_down, precision=precise) + down_bias)
    return middle + branch_two

def reference(cell_input, cotangent, segment_ids, lengths, w_qkv, query_bias, value_bias, w_out, out_bias, w_up, up_bias, w_down, down_bias, norm1_gain, norm1_bias, norm2_gain, norm2_bias):
    params = tuple((p.astype(jnp.float32) for p in (w_qkv, query_bias, value_bias, w_out, out_bias, w_up, up_bias, w_down, down_bias, norm1_gain, norm1_bias, norm2_gain, norm2_bias)))
    group_size = math.gcd(SEQS, max(1, 2048 // TOK_DEV))
    group_count = SEQS // group_size
    pos_table = positions(TOK_DEV, D)
    places = jnp.arange(TOK_DEV, dtype=jnp.int32)
    cells_f = cell_input.astype(jnp.float32).reshape(group_count, group_size, TOK_DEV, D)
    grads_f = cotangent.astype(jnp.float32).reshape(group_count, group_size, TOK_DEV, D)
    seg_groups = segment_ids.reshape(group_count, group_size, TOK_DEV)
    len_groups = lengths.reshape(group_count, group_size)

    def scan_step(running, inputs):
        block_in, block_grad, seg_block, len_block = inputs
        live_cells = places[None, :] < len_block[:, None]
        same_slide = seg_block[:, :, None] == seg_block[:, None, :]
        allowed = same_slide & live_cells[:, :, None] & live_cells[:, None, :] | (places[:, None] == places[None, :])[None]
        result, pullback = jax.vjp(lambda p, c: block(p, c, pos_table, allowed), params, block_in)
        grad_params, grad_cells = pullback(block_grad)
        running = tuple((a + b for a, b in zip(running, grad_params)))
        return (running, (result.astype(jnp.bfloat16), grad_cells.astype(jnp.bfloat16)))
    zero_grads = tuple((jnp.zeros_like(p) for p in params))
    totals, (results, cell_grads) = lax.scan(scan_step, zero_grads, (cells_f, grads_f, seg_groups, len_groups))
    block_out = results.reshape(TOKENS, D)
    input_grad = cell_grads.reshape(TOKENS, D)
    return (block_out, input_grad, totals[0], totals[1], totals[2], totals[3], totals[4], totals[5], totals[6], totals[7], totals[8], totals[9], totals[10], totals[11], totals[12])
```

```python
import math

import jax
import jax.numpy as jnp
from jax import lax
from jax.sharding import PartitionSpec as P

HEAD_DIM = 64


def normalize(values_in):
    row_mean = jnp.mean(values_in, axis=-1, keepdims=True)
    centred = values_in - row_mean
    inv_std = lax.rsqrt(jnp.mean(centred * centred, axis=-1, keepdims=True) + 1e-05)
    return (centred * inv_std, inv_std)


def norm_back(incoming, normed, inv_std, gain_vec):
    scaled = incoming * gain_vec
    return inv_std * (
        scaled
        - jnp.mean(scaled, axis=-1, keepdims=True)
        - normed * jnp.mean(scaled * normed, axis=-1, keepdims=True)
    )


def positions(length, model_width):
    places = jnp.arange(length, dtype=jnp.float32)[:, None]
    frequency = jnp.exp(
        jnp.arange(model_width // 2, dtype=jnp.float32) * (-2.0 * math.log(10000.0) / model_width)
    )
    angles = places * frequency[None, :]
    return jnp.stack([jnp.sin(angles), jnp.cos(angles)], axis=-1).reshape(length, model_width)


def gelu_slope(values_in):
    normal_cdf = 0.5 * (1.0 + lax.erf(values_in * (1.0 / math.sqrt(2.0))))
    return normal_cdf + values_in * jnp.exp(-0.5 * values_in * values_in) * (
        1.0 / math.sqrt(2.0 * math.pi)
    )


def block_mask(begin_row, block_rows, seg_row, live_cells):
    places = jnp.arange(seg_row.shape[0], dtype=jnp.int32)
    rows_at = begin_row + jnp.arange(block_rows, dtype=jnp.int32)
    return (seg_row[:, None] == seg_row[None, :]) & live_cells[:, None] & live_cells[None, :] | (
        rows_at[:, None] == places[None, :]
    )


def masked_scores(block_q, key_vecs, begin_row, block_rows, seg_row, live_cells):
    score_scale = 1.0 / math.sqrt(HEAD_DIM)
    scores = (
        jnp.einsum("qhd,khd->hqk", block_q, key_vecs, preferred_element_type=jnp.float32)
        * score_scale
    )
    return jnp.where(block_mask(begin_row, block_rows, seg_row, live_cells)[None], scores, -1e30)


def attention_forward(queries, key_vecs, values, seg_row, live_cells, block_rows):
    begin_rows = jnp.arange(queries.shape[0] // block_rows, dtype=jnp.int32) * block_rows

    def query_block(begin_row):
        scores = masked_scores(queries, key_vecs, begin_row, block_rows, seg_row, live_cells)
        row_max = jnp.max(scores, axis=-1, keepdims=True)
        exp_scores = jnp.exp(scores - row_max)
        row_total = jnp.sum(exp_scores, axis=-1, keepdims=True)
        weights = (exp_scores / row_total).astype(jnp.bfloat16)
        attended = jnp.einsum("hqk,khd->qhd", weights, values, preferred_element_type=jnp.float32)
        return (attended.astype(jnp.bfloat16), (row_max + jnp.log(row_total))[..., 0])

    attended, log_totals = lax.map(query_block, begin_rows)
    return (attended.reshape(queries.shape), log_totals)


def attention_backward(
    queries, key_vecs, values, attended_grad, log_totals, seg_row, live_cells, block_rows
):
    score_scale = 1.0 / math.sqrt(HEAD_DIM)
    begin_rows = jnp.arange(queries.shape[0] // block_rows, dtype=jnp.int32) * block_rows

    def query_block(running, inputs):
        begin_row, block_log = inputs
        key_total, value_total = running
        scores = masked_scores(queries, key_vecs, begin_row, block_rows, seg_row, live_cells)
        weights_f = jnp.exp(scores - block_log[..., None])
        value_total = value_total + jnp.einsum(
            "hqk,qhd->khd",
            weights_f.astype(jnp.bfloat16),
            attended_grad,
            preferred_element_type=jnp.float32,
        )
        prob_grad = jnp.einsum(
            "qhd,khd->hqk", attended_grad, values, preferred_element_type=jnp.float32
        )
        dscore = (
            weights_f * (prob_grad - jnp.sum(prob_grad * weights_f, axis=-1, keepdims=True))
        ).astype(jnp.bfloat16)
        block_dq = (
            jnp.einsum("hqk,khd->qhd", dscore, key_vecs, preferred_element_type=jnp.float32)
            * score_scale
        ).astype(jnp.bfloat16)
        key_total = (
            key_total
            + jnp.einsum("hqk,qhd->khd", dscore, queries, preferred_element_type=jnp.float32)
            * score_scale
        )
        return ((key_total, value_total), block_dq)

    zero_acc = jnp.zeros(queries.shape, jnp.float32)
    (key_total, value_total), query_grad = lax.scan(
        query_block, (zero_acc, zero_acc), (begin_rows, log_totals)
    )
    return (
        query_grad.reshape(queries.shape),
        key_total.astype(jnp.bfloat16),
        value_total.astype(jnp.bfloat16),
    )


def forward_pass(gathered, cell_input, pos_table, seg_row, live_cells, block_rows):
    (
        w_qkv,
        query_bias,
        value_bias,
        w_out,
        out_bias,
        w_up,
        up_bias,
        w_down,
        down_bias,
        norm1_gain,
        norm1_bias,
        norm2_gain,
        norm2_bias,
    ) = gathered
    length, model_width = cell_input.shape
    head_count = model_width // HEAD_DIM
    cells_f = cell_input.astype(jnp.float32)
    normed_one, inv_one = normalize(cells_f)
    normed_in = (
        normed_one * norm1_gain.astype(jnp.float32) + norm1_bias.astype(jnp.float32) + pos_table
    ).astype(jnp.bfloat16)
    projected = jnp.dot(normed_in, w_qkv, preferred_element_type=jnp.float32)
    queries = (
        (projected[:, :model_width] + query_bias.astype(jnp.float32))
        .astype(jnp.bfloat16)
        .reshape(length, head_count, HEAD_DIM)
    )
    key_vecs = (
        projected[:, model_width : 2 * model_width]
        .astype(jnp.bfloat16)
        .reshape(length, head_count, HEAD_DIM)
    )
    values = (
        (projected[:, 2 * model_width :] + value_bias.astype(jnp.float32))
        .astype(jnp.bfloat16)
        .reshape(length, head_count, HEAD_DIM)
    )
    attended, log_totals = attention_forward(
        queries, key_vecs, values, seg_row, live_cells, block_rows
    )
    attended = attended.reshape(length, model_width)
    middle = (
        cells_f
        + jnp.dot(attended, w_out, preferred_element_type=jnp.float32)
        + out_bias.astype(jnp.float32)
    )
    normed_two, inv_two = normalize(middle)
    hidden_in = (
        normed_two * norm2_gain.astype(jnp.float32) + norm2_bias.astype(jnp.float32)
    ).astype(jnp.bfloat16)
    pre_act = jnp.dot(hidden_in, w_up, preferred_element_type=jnp.float32) + up_bias.astype(
        jnp.float32
    )
    hidden = jax.nn.gelu(pre_act, approximate=False).astype(jnp.bfloat16)
    result = (
        middle
        + jnp.dot(hidden, w_down, preferred_element_type=jnp.float32)
        + down_bias.astype(jnp.float32)
    )
    kept = (
        normed_in,
        normed_one,
        inv_one,
        queries,
        key_vecs,
        values,
        attended,
        log_totals,
        normed_two,
        inv_two,
        hidden_in,
        pre_act,
        hidden,
    )
    return (result.astype(jnp.bfloat16), kept)


def backward_pass(gathered, kept, cotangent, seg_row, live_cells, block_rows):
    (
        w_qkv,
        query_bias,
        value_bias,
        w_out,
        out_bias,
        w_up,
        up_bias,
        w_down,
        down_bias,
        norm1_gain,
        norm1_bias,
        norm2_gain,
        norm2_bias,
    ) = gathered
    (
        normed_in,
        normed_one,
        inv_one,
        queries,
        key_vecs,
        values,
        attended,
        log_totals,
        normed_two,
        inv_two,
        hidden_in,
        pre_act,
        hidden,
    ) = kept
    length = attended.shape[0]
    upstream = cotangent.astype(jnp.float32)
    grad_down = jnp.einsum("tf,td->fd", hidden, cotangent, preferred_element_type=jnp.float32)
    grad_down_bias = jnp.sum(upstream, axis=0)
    hidden_grad = jnp.einsum("td,fd->tf", cotangent, w_down, preferred_element_type=jnp.float32)
    pre_grad = (hidden_grad * gelu_slope(pre_act)).astype(jnp.bfloat16)
    grad_up = jnp.einsum("td,tf->df", hidden_in, pre_grad, preferred_element_type=jnp.float32)
    grad_up_bias = jnp.sum(pre_grad.astype(jnp.float32), axis=0)
    mid_grad = jnp.einsum("tf,df->td", pre_grad, w_up, preferred_element_type=jnp.float32)
    grad_gain_two = jnp.sum(mid_grad * normed_two, axis=0)
    grad_shift_two = jnp.sum(mid_grad, axis=0)
    middle_grad = upstream + norm_back(
        mid_grad, normed_two, inv_two, norm2_gain.astype(jnp.float32)
    )
    branch_grad = middle_grad.astype(jnp.bfloat16)
    grad_out = jnp.einsum("td,te->de", attended, branch_grad, preferred_element_type=jnp.float32)
    grad_out_bias = jnp.sum(branch_grad.astype(jnp.float32), axis=0)
    attended_grad = jnp.einsum(
        "te,de->td", branch_grad, w_out, preferred_element_type=jnp.float32
    ).astype(jnp.bfloat16)
    query_grad, key_grad, value_grad = attention_backward(
        queries,
        key_vecs,
        values,
        attended_grad.reshape(queries.shape),
        log_totals,
        seg_row,
        live_cells,
        block_rows,
    )
    query_grad = query_grad.reshape(length, -1)
    value_grad = value_grad.reshape(length, -1)
    proj_grad = jnp.concatenate([query_grad, key_grad.reshape(length, -1), value_grad], axis=1)
    grad_qkv = jnp.einsum("td,te->de", normed_in, proj_grad, preferred_element_type=jnp.float32)
    grad_query_bias = jnp.sum(query_grad.astype(jnp.float32), axis=0)
    grad_value_bias = jnp.sum(value_grad.astype(jnp.float32), axis=0)
    in_grad = jnp.einsum("te,de->td", proj_grad, w_qkv, preferred_element_type=jnp.float32)
    grad_gain_one = jnp.sum(in_grad * normed_one, axis=0)
    grad_shift_one = jnp.sum(in_grad, axis=0)
    input_grad = (
        middle_grad + norm_back(in_grad, normed_one, inv_one, norm1_gain.astype(jnp.float32))
    ).astype(jnp.bfloat16)
    grads = (
        grad_qkv,
        grad_query_bias,
        grad_value_bias,
        grad_out,
        grad_out_bias,
        grad_up,
        grad_up_bias,
        grad_down,
        grad_down_bias,
        grad_gain_one,
        grad_shift_one,
        grad_gain_two,
        grad_shift_two,
    )
    return (input_grad, grads)


VECTORS = (1, 2, 4, 6, 8, 9, 10, 11, 12)
MATRICES = (0, 3, 5, 7)
EVERY = ("dp", "rep")


def gather_matrix(shard):
    part_rows = shard.shape[0] // lax.axis_size("rep")
    own = lax.dynamic_slice_in_dim(shard, lax.axis_index("rep") * part_rows, part_rows, 0)
    return lax.all_gather(own, EVERY, axis=0, tiled=True)


def gather_vectors(shards):
    packed = jnp.concatenate(shards)
    whole = lax.all_gather(packed, "dp", axis=0, tiled=False)
    vectors, begin = [], 0
    for shard in shards:
        vectors.append(whole[:, begin : begin + shard.shape[0]].reshape(-1))
        begin += shard.shape[0]
    return vectors


def reduce_matrix(grad):
    part = lax.psum_scatter(grad.astype(jnp.bfloat16), EVERY, scatter_dimension=0, tiled=True)
    return lax.all_gather(part, "rep", axis=0, tiled=True).astype(jnp.float32)


def reduce_vectors(grads):
    owners = lax.axis_size("dp")
    packed = jnp.concatenate([grad.reshape(owners, -1) for grad in grads], axis=1)
    total = lax.psum(packed, EVERY)
    own = lax.dynamic_index_in_dim(total, lax.axis_index("dp"), 0, keepdims=False)
    outs, begin = [], 0
    for grad in grads:
        size = grad.shape[0] // owners
        outs.append(own[begin : begin + size])
        begin += size
    return outs


def on_device(
    cell_input,
    cotangent,
    segment_ids,
    lengths,
    *shards,
):
    gathered = [None] * len(shards)
    for place, vector in zip(VECTORS, gather_vectors([shards[place] for place in VECTORS])):
        gathered[place] = vector
    for place in MATRICES:
        gathered[place] = gather_matrix(shards[place])
    length, model_width = cell_input.shape
    block_rows = min(length, 512)
    seg_row = segment_ids[0]
    live_cells = jnp.arange(length, dtype=jnp.int32) < lengths[0]
    pos_table = positions(length, model_width)
    block_out, kept = forward_pass(
        gathered, cell_input, pos_table, seg_row, live_cells, block_rows
    )
    input_grad, grads = backward_pass(gathered, kept, cotangent, seg_row, live_cells, block_rows)
    summed = [None] * len(grads)
    for place in (7, 5, 3, 0):
        summed[place] = reduce_matrix(grads[place])
    for place, vector in zip(VECTORS, reduce_vectors([grads[place] for place in VECTORS])):
        summed[place] = vector
    return (block_out, input_grad) + tuple(summed)


def solution(mesh):
    in_specs = (
        P(("dp", "rep"), None),
        P(("dp", "rep"), None),
        P(("dp", "rep"), None),
        P(("dp", "rep")),
        P("dp", None),
        P("dp"),
        P("dp"),
        P("dp", None),
        P("dp"),
        P("dp", None),
        P("dp"),
        P("dp", None),
        P("dp"),
        P("dp"),
        P("dp"),
        P("dp"),
        P("dp"),
    )
    out_specs = (
        P(("dp", "rep"), None),
        P(("dp", "rep"), None),
        P("dp", None),
        P("dp"),
        P("dp"),
        P("dp", None),
        P("dp"),
        P("dp", None),
        P("dp"),
        P("dp", None),
        P("dp"),
        P("dp"),
        P("dp"),
        P("dp"),
        P("dp"),
    )
    return jax.shard_map(
        on_device, mesh=mesh, in_specs=in_specs, out_specs=out_specs, check_vma=False
    )
```

```python
import math

import jax
import jax.numpy as jnp
from jax import lax
from jax.sharding import PartitionSpec as P

HEAD_DIM = 64


def normalize(values_in):
    row_mean = jnp.mean(values_in, axis=-1, keepdims=True)
    centred = values_in - row_mean
    inv_std = lax.rsqrt(jnp.mean(centred * centred, axis=-1, keepdims=True) + 1e-05)
    return (centred * inv_std, inv_std)


def norm_back(incoming, normed, inv_std, gain_vec):
    scaled = incoming * gain_vec
    return inv_std * (
        scaled
        - jnp.mean(scaled, axis=-1, keepdims=True)
        - normed * jnp.mean(scaled * normed, axis=-1, keepdims=True)
    )


def positions(length, model_width):
    places = jnp.arange(length, dtype=jnp.float32)[:, None]
    frequency = jnp.exp(
        jnp.arange(model_width // 2, dtype=jnp.float32) * (-2.0 * math.log(10000.0) / model_width)
    )
    angles = places * frequency[None, :]
    return jnp.stack([jnp.sin(angles), jnp.cos(angles)], axis=-1).reshape(length, model_width)


def gelu_slope(values_in):
    normal_cdf = 0.5 * (1.0 + lax.erf(values_in * (1.0 / math.sqrt(2.0))))
    return normal_cdf + values_in * jnp.exp(-0.5 * values_in * values_in) * (
        1.0 / math.sqrt(2.0 * math.pi)
    )


def allowed_pairs(segments, live):
    places = jnp.arange(segments.shape[1], dtype=jnp.int32)
    alive = places[None, :] < live[:, None]
    same = segments[:, :, None] == segments[:, None, :]
    return (same & alive[:, :, None] & alive[:, None, :]) | (
        places[:, None] == places[None, :]
    )


def masked_scores(queries, key_vecs, segments, live):
    scores = jnp.einsum("sqhd,skhd->shqk", queries, key_vecs, preferred_element_type=jnp.float32)
    scores = scores * (1.0 / math.sqrt(HEAD_DIM))
    return jnp.where(allowed_pairs(segments, live)[:, None], scores, -1e30)


def attention_forward(queries, key_vecs, values, segments, live):
    scores = masked_scores(queries, key_vecs, segments, live)
    row_max = jnp.max(scores, axis=-1, keepdims=True)
    exp_scores = jnp.exp(scores - row_max)
    row_total = jnp.sum(exp_scores, axis=-1, keepdims=True)
    weights = (exp_scores / row_total).astype(jnp.bfloat16)
    attended = jnp.einsum("shqk,skhd->sqhd", weights, values, preferred_element_type=jnp.float32)
    return attended.astype(jnp.bfloat16), row_max + jnp.log(row_total)


def attention_backward(queries, key_vecs, values, attended_grad, log_totals, segments, live):
    score_scale = 1.0 / math.sqrt(HEAD_DIM)
    scores = masked_scores(queries, key_vecs, segments, live)
    weights_f = jnp.exp(scores - log_totals)
    value_grad = jnp.einsum(
        "shqk,sqhd->skhd",
        weights_f.astype(jnp.bfloat16),
        attended_grad,
        preferred_element_type=jnp.float32,
    )
    prob_grad = jnp.einsum(
        "sqhd,skhd->shqk", attended_grad, values, preferred_element_type=jnp.float32
    )
    dscore = (
        weights_f * (prob_grad - jnp.sum(prob_grad * weights_f, axis=-1, keepdims=True))
    ).astype(jnp.bfloat16)
    query_grad = jnp.einsum("shqk,skhd->sqhd", dscore, key_vecs, preferred_element_type=jnp.float32)
    key_grad = jnp.einsum("shqk,sqhd->skhd", dscore, queries, preferred_element_type=jnp.float32)
    return (
        (query_grad * score_scale).astype(jnp.bfloat16),
        (key_grad * score_scale).astype(jnp.bfloat16),
        value_grad.astype(jnp.bfloat16),
    )


EVERY = ("dp", "rep")
CORE, SIDE = 1, 2


def split_bits():
    rep = lax.axis_size("rep")
    owners = lax.axis_size("dp")
    bits = [rep << place for place in range(owners.bit_length() - 1)]
    return bits[0], bits[1:]


def swap(value, bit):
    count = lax.axis_size("dp") * lax.axis_size("rep")
    return lax.ppermute(value, EVERY, [(i, i ^ bit) for i in range(count)])


def bit_of(bit):
    return (lax.axis_index(EVERY) & bit) // bit


def take(value, bit, axis, other=False):
    at = bit_of(bit)
    return lax.dynamic_index_in_dim(value, 1 - at if other else at, axis, keepdims=False)


def merge(own, got, bit, axis):
    high = bit_of(bit) == 1
    return jnp.stack([jnp.where(high, got, own), jnp.where(high, own, got)], axis=axis)


def low(value):
    return value.astype(jnp.bfloat16)


def added(*values):
    return low(sum(value.astype(jnp.float32) for value in values))


def gather_far(own, far_bits):
    rows, columns = own.shape
    own = own[None]
    for bit in far_bits:
        own = merge(own, swap(own, bit), bit, 0).reshape(-1, rows, columns)
    return own


def gather_quarter(own, near_bit, far_bits):
    columns = own.shape[1]
    own = gather_far(own, far_bits)
    first, second = own[:, :, : columns // 2], own[:, :, columns // 2 :]
    second = jnp.stack([second, swap(second, SIDE)])
    first = merge(first, swap(first, near_bit), near_bit, 1).reshape(-1, columns // 2)
    second = merge(second, swap(second, near_bit), near_bit, 2).reshape(2, -1, columns // 2)
    return (
        jnp.concatenate([first, second[0]], axis=1),
        jnp.concatenate([swap(first, SIDE), second[1]], axis=1),
    )


def gather_half(own, near_bit, far_bits):
    columns = own.shape[1]
    own = gather_far(own, far_bits)
    return merge(own, swap(own, near_bit), near_bit, 1).reshape(-1, columns)


def reduce_far(value, far_bits):
    for bit in reversed(far_bits):
        value = value.reshape((2, -1) + value.shape[1:])
        value = added(take(value, bit, 0), swap(take(value, bit, 0, True), bit))
    return value[0]


def reduce_quarter(own, other, near_bit, far_bits):
    owners = lax.axis_size("dp")
    columns = own.shape[1]
    own = own.reshape(owners // 2, 2, -1, columns)
    other = other.reshape(own.shape)
    half = columns // 2
    first = jnp.stack([own[..., :half], other[..., :half]])
    got = swap(take(first, near_bit, 2, True), near_bit)
    second = added(own[..., half:], swap(other[..., half:], SIDE))
    first = added(take(first, near_bit, 2), got)
    got = swap(take(second, near_bit, 1, True), near_bit)
    first = added(first[0], swap(first[1], SIDE))
    second = added(take(second, near_bit, 1), got)
    return reduce_far(jnp.concatenate([first, second], axis=-1), far_bits)


def spread_quarter(own):
    pair = merge(own, swap(own, CORE), CORE, 0)
    pair = merge(pair, swap(pair, SIDE), SIDE, 0)
    return [pair[at // 2, at % 2] for at in range(4)]


def reduce_half(own, near_bit, far_bits):
    owners = lax.axis_size("dp")
    own = own.reshape(owners // 2, 2, -1, own.shape[1])
    own = added(take(own, near_bit, 1), swap(take(own, near_bit, 1, True), near_bit))
    own = reduce_far(own, far_bits)
    return added(own, swap(own, SIDE))


def gather_vectors(shards, near_bit, far_bits):
    packed = jnp.concatenate(shards)[None]
    whole = gather_half(packed, near_bit, far_bits)
    vectors, begin = [], 0
    for shard in shards:
        vectors.append(whole[:, begin : begin + shard.shape[0]].reshape(-1))
        begin += shard.shape[0]
    return vectors


def reduce_vectors(grads, near_bit, far_bits):
    owners = lax.axis_size("dp")
    value = jnp.concatenate([grad.reshape(owners, -1) for grad in grads], axis=1)
    value = value.reshape(owners // 2, 2, -1)
    value = take(value, near_bit, 1) + swap(take(value, near_bit, 1, True), near_bit)
    for bit in reversed(far_bits):
        value = value.reshape(2, -1, value.shape[-1])
        value = take(value, bit, 0) + swap(take(value, bit, 0, True), bit)
    value = value[0]
    for bit in (CORE, SIDE):
        value = value + swap(value, bit)
    outs, begin = [], 0
    for grad in grads:
        size = grad.shape[0] // owners
        outs.append(value[begin : begin + size])
        begin += size
    return outs


def quarter_columns(shard, groups, width, at):
    step = 4 * width
    return jnp.concatenate(
        [
            lax.dynamic_slice_in_dim(shard, group * step + at * width, width, shard.ndim - 1)
            for group in range(groups)
        ],
        axis=-1,
    )


def join_quarters(parts, groups, width):
    return jnp.concatenate(
        [
            part[..., group * width : (group + 1) * width]
            for group in range(groups)
            for part in parts
        ],
        axis=-1,
    )


def both(own):
    return jnp.concatenate([own, swap(own, CORE)])


def on_device(
    cell_input,
    cotangent,
    segment_ids,
    lengths,
    w_qkv,
    query_bias,
    value_bias,
    w_out,
    out_bias,
    w_up,
    up_bias,
    w_down,
    down_bias,
    norm1_gain,
    norm1_bias,
    norm2_gain,
    norm2_bias,
):
    near_bit, far_bits = split_bits()
    owners = lax.axis_size("dp")
    place = lax.axis_index("rep")
    length, width = cell_input.shape
    quarter = width // 4
    head_count = width // HEAD_DIM // 2
    piece = w_down.shape[0] // 4

    heads_at = (place % 2) * 2 + place // 2
    (
        query_bias,
        value_bias,
        out_bias,
        up_bias,
        down_bias,
        norm1_gain,
        norm1_bias,
        norm2_gain,
        norm2_bias,
    ) = [
        vector.astype(jnp.float32)
        for vector in gather_vectors(
            [
                query_bias,
                value_bias,
                out_bias,
                up_bias,
                down_bias,
                norm1_gain,
                norm1_bias,
                norm2_gain,
                norm2_bias,
            ],
            near_bit,
            far_bits,
        )
    ]
    qkv_own, qkv_other = gather_quarter(
        quarter_columns(w_qkv, 3, quarter, heads_at), near_bit, far_bits
    )
    out_half = gather_half(
        lax.dynamic_slice_in_dim(w_out, (place % 2) * (width // 2), width // 2, 1),
        near_bit,
        far_bits,
    )
    out_whole = merge(out_half, swap(out_half, CORE), CORE, 1).reshape(width, width)
    up_own, up_other = gather_quarter(
        quarter_columns(w_up, owners, piece, place), near_bit, far_bits
    )
    down_own, down_other = gather_quarter(
        lax.dynamic_slice_in_dim(w_down, place * piece, piece, 0), near_bit, far_bits
    )
    side_at = place // 2

    def relative(natural):
        split = natural.reshape(natural.shape[:-1] + (2, 2, quarter))
        halves = []
        for other_core in (False, True):
            half = take(split, CORE, split.ndim - 3, other_core)
            swapped = jnp.where(side_at == 1, half[..., 1, :], half[..., 0, :])
            rest = jnp.where(side_at == 1, half[..., 0, :], half[..., 1, :])
            halves.append(jnp.concatenate([swapped, rest], axis=-1))
        return halves

    def natural(mine, theirs):
        halves = []
        for half in (mine, theirs):
            first, second = half[..., :quarter], half[..., quarter:]
            halves.append(
                jnp.concatenate(
                    [
                        jnp.where(side_at == 1, second, first),
                        jnp.where(side_at == 1, first, second),
                    ],
                    axis=-1,
                )
            )
        mine, theirs = halves
        high = place % 2 == 1
        return jnp.concatenate(
            [jnp.where(high, theirs, mine), jnp.where(high, mine, theirs)], axis=-1
        )

    def dot(left, right):
        return jnp.dot(left, right, preferred_element_type=jnp.float32)

    def dot_t(left, right):
        return lax.dot_general(
            left, right, (((1,), (1,)), ((), ())), preferred_element_type=jnp.float32
        )

    def over_rows(left, right):
        return lax.dot_general(
            left, right, (((0,), (0,)), ((), ())), preferred_element_type=jnp.float32
        )

    cells = both(cell_input)
    upstream = both(cotangent)
    segments = both(segment_ids)
    live = jnp.concatenate([lengths, swap(lengths, CORE)])
    pos_table = positions(length, width)
    normed_one, inv_one = normalize(cells.astype(jnp.float32))
    normed_in = low(
        (normed_one * norm1_gain + norm1_bias).reshape(2, length, width) + pos_table
    ).reshape(2 * length, width)
    normed_one, inv_one = normed_one[:length], inv_one[:length]
    cells_f = cell_input.astype(jnp.float32)

    bias_q, bias_v = relative(query_bias)[0], relative(value_bias)[0]
    proj_own = dot(normed_in, qkv_own)
    proj_other = dot(normed_in, qkv_other)

    def heads(at, bias):
        value = jnp.concatenate(
            [
                proj_own[:, at * quarter : (at + 1) * quarter],
                proj_other[:, at * quarter : (at + 1) * quarter],
            ],
            axis=1,
        )
        if bias is not None:
            value = value + bias
        return low(value).reshape(2, length, head_count, HEAD_DIM)

    queries, key_vecs, values = heads(0, bias_q), heads(1, None), heads(2, bias_v)
    attended, probs_kept = attention_forward(queries, key_vecs, values, segments, live)
    attended = attended.reshape(2, length, width // 2)
    attended = natural(attended[0], swap(attended[1], CORE))
    middle = cells_f + dot(attended, out_whole) + out_bias
    normed_two, inv_two = normalize(middle)
    hidden_in = both(low(normed_two * norm2_gain + norm2_bias))

    hidden, slopes = [], []
    for weight, at in ((up_own, place), (up_other, place ^ SIDE)):
        pre_act = dot(hidden_in, weight) + quarter_columns(up_bias, owners, piece, at)
        hidden.append(low(jax.nn.gelu(pre_act, approximate=False)))
        slopes.append(gelu_slope(pre_act))
    partial = dot(hidden[0], down_own) + dot(hidden[1], down_other)
    block_out = low(
        middle + partial[:length] + swap(low(partial[length:]), CORE).astype(jnp.float32) + down_bias
    )

    pre_grads = [
        low(dot_t(upstream, weight) * slope)
        for weight, slope in zip((down_own, down_other), slopes)
    ]
    grad_down = reduce_quarter(
        *[low(over_rows(part, upstream)) for part in hidden], near_bit, far_bits
    )
    grad_up = reduce_quarter(
        *[low(over_rows(hidden_in, part)) for part in pre_grads], near_bit, far_bits
    )
    mid_partial = dot_t(pre_grads[0], up_own) + dot_t(pre_grads[1], up_other)
    mid_grad = mid_partial[:length] + swap(low(mid_partial[length:]), CORE).astype(jnp.float32)
    up_bias_grads = [jnp.sum(part.astype(jnp.float32), axis=0) for part in pre_grads]
    own_g = cotangent.astype(jnp.float32)
    middle_grad = own_g + norm_back(mid_grad, normed_two, inv_two, norm2_gain)
    branch_grad = low(middle_grad)
    grad_out = over_rows(attended, branch_grad).reshape(width, 2, width // 2)
    grad_out = low(grad_out)
    grad_out = added(take(grad_out, CORE, 1), swap(take(grad_out, CORE, 1, True), CORE))
    grad_out = reduce_half(grad_out, near_bit, far_bits)
    attended_grad = low(dot_t(branch_grad, out_whole))
    mine, theirs = relative(attended_grad)
    attended_grad = jnp.stack([mine, swap(theirs, CORE)]).reshape(queries.shape)
    query_grad, key_grad, value_grad = [
        part.reshape(2 * length, width // 2)
        for part in attention_backward(
            queries, key_vecs, values, attended_grad, probs_kept, segments, live
        )
    ]
    proj_grads = [
        jnp.concatenate([part[:, at : at + quarter] for part in (query_grad, key_grad, value_grad)], axis=1)
        for at in (0, quarter)
    ]
    grad_qkv = reduce_quarter(
        *[low(over_rows(normed_in, part)) for part in proj_grads], near_bit, far_bits
    )
    in_partial = dot_t(proj_grads[0], qkv_own) + dot_t(proj_grads[1], qkv_other)
    in_grad = in_partial[:length] + swap(low(in_partial[length:]), CORE).astype(jnp.float32)
    input_grad = low(middle_grad + norm_back(in_grad, normed_one, inv_one, norm1_gain))

    def head_sums(part):
        sums = jnp.sum(part.astype(jnp.float32), axis=0)
        return natural(sums, jnp.zeros_like(sums))

    up_at = jnp.arange(4)[None, :, None]
    up_bias_grad = sum(
        jnp.where(up_at == at, part.reshape(owners, 1, piece), 0.0)
        for part, at in zip(up_bias_grads, (place, place ^ SIDE))
    ).reshape(-1)
    (
        grad_query_bias,
        grad_value_bias,
        grad_out_bias,
        grad_up_bias,
        grad_down_bias,
        grad_norm1_gain,
        grad_norm1_bias,
        grad_norm2_gain,
        grad_norm2_bias,
    ) = reduce_vectors(
        [
            head_sums(query_grad),
            head_sums(value_grad),
            jnp.sum(branch_grad.astype(jnp.float32), axis=0),
            up_bias_grad,
            jnp.sum(own_g, axis=0),
            jnp.sum(in_grad * normed_one, axis=0),
            jnp.sum(in_grad, axis=0),
            jnp.sum(mid_grad * normed_two, axis=0),
            jnp.sum(mid_grad, axis=0),
        ],
        near_bit,
        far_bits,
    )
    down_parts = spread_quarter(grad_down)
    up_parts = spread_quarter(grad_up)
    qkv_parts = spread_quarter(grad_qkv)
    heads_order = [qkv_parts[at] for at in (0, 2, 1, 3)]
    return (
        block_out,
        input_grad,
        join_quarters(heads_order, 3, quarter).astype(jnp.float32),
        grad_query_bias,
        grad_value_bias,
        merge(grad_out, swap(grad_out, CORE), CORE, 1).reshape(-1, width).astype(jnp.float32),
        grad_out_bias,
        join_quarters(up_parts, owners, piece).astype(jnp.float32),
        grad_up_bias,
        jnp.concatenate(down_parts).astype(jnp.float32),
        grad_down_bias,
        grad_norm1_gain,
        grad_norm1_bias,
        grad_norm2_gain,
        grad_norm2_bias,
    )


def solution(mesh):
    in_specs = (
        P(("dp", "rep"), None),
        P(("dp", "rep"), None),
        P(("dp", "rep"), None),
        P(("dp", "rep")),
        P("dp", None),
        P("dp"),
        P("dp"),
        P("dp", None),
        P("dp"),
        P("dp", None),
        P("dp"),
        P("dp", None),
        P("dp"),
        P("dp"),
        P("dp"),
        P("dp"),
        P("dp"),
    )
    out_specs = (
        P(("dp", "rep"), None),
        P(("dp", "rep"), None),
        P("dp", None),
        P("dp"),
        P("dp"),
        P("dp", None),
        P("dp"),
        P("dp", None),
        P("dp"),
        P("dp", None),
        P("dp"),
        P("dp"),
        P("dp"),
        P("dp"),
        P("dp"),
    )
    return jax.shard_map(
        on_device, mesh=mesh, in_specs=in_specs, out_specs=out_specs, check_vma=False
    )
```
